32 devices in a mesh: grp: 4 (over z), sub: 8 (over y, x, core).
Axes of the slice: x: 2, y: 2, z: 4, core: 2. Of those that a mesh axis runs over, the one named last changes fastest.
Arguments:
- activations: bfloat16 [49152, 2048], P(('grp', 'sub')), may hold values from -16 to 16, as said below
- cotangent: bfloat16 [49152, 1024], P(('grp', 'sub')), may hold values from -16 to 16, as said below
- weight: bfloat16 [2048, 1024], replicated, may hold values from -0.125 to 0.125
- master: float32 [2048, 1024], P(('grp', 'sub')), may hold values from -1.5 to 1.5
- momentum: float32 [2048, 1024], P(('grp', 'sub')), may hold values from -6 to 6
Outputs:
- input_grad: bfloat16 [49152, 2048], P(('grp', 'sub'))
- new_momentum: float32 [2048, 1024], P(('grp', 'sub'))
- new_master: float32 [2048, 1024], P(('grp', 'sub'))
- new_weight: bfloat16 [2048, 1024], replicated
The draws below stay inside these ranges and needn't reach their ends.
Inputs may be any that keep to these rules, and one draw needn't show every extreme that they name: `activations`: activations of the kind a projection receives. `cotangent`: gradients of the kind a loss gives.
All inputs are finite; a program needn't handle non-finite values.
Results may differ from the reference program's by a relative error of at most 0.001.
Values may be sent and summed in bfloat16 or wider, within the bound.
No kernel may reach another device: no remote copies, remote signals or barrier semaphores. Data moves between devices by JAX's collectives and lax.ppermute only.
A program may use at most 128 MiB of HBM per device.

```python
import jax
import jax.numpy as jnp
from jax import lax

D = 2048
KV = 1024
TOK_DEV = 1536
N_GRP = 4
N_SUB = 8


def shaped_draw(key, width, tag):
    group_rows = TOK_DEV * N_SUB
    base_key = jax.random.fold_in(key, tag)
    common = jax.random.normal(jax.random.fold_in(base_key, 1), (group_rows, width), jnp.float32)
    spread = jnp.exp(jax.random.uniform(jax.random.fold_in(base_key, 4), (width,), jnp.float32, jnp.log(0.3), jnp.log(3.0)))
    noise = jax.random.normal(jax.random.fold_in(base_key, 2), (N_GRP, group_rows, width), jnp.float32)
    weights = jax.random.uniform(jax.random.fold_in(base_key, 3), (N_GRP, 1, 1), jnp.float32, 0.6, 1.4)
    steps = jnp.arange(N_GRP, dtype=jnp.float32) / max(N_GRP - 1, 1)
    rising = (0.2 * jnp.power(3.0, steps))[:, None, None]
    ramp = jnp.power(3.0, jnp.arange(width, dtype=jnp.float32) / width)
    values = (weights * common[None] + rising * noise) * (spread * ramp)
    values = jnp.clip(values, -16.0, 16.0)
    return values.reshape(N_GRP * group_rows, width).astype(jnp.bfloat16)


def draw_activations(key, part):
    return shaped_draw(key, D, 11)


def draw_cotangent(key, part):
    return shaped_draw(key, KV, 23)


def block_scale(key, dims, shards, low, high):
    loudness = 1.0
    for axis_at, shards_of in shards:
        heights = jax.random.uniform(jax.random.fold_in(jax.random.fold_in(key, 6), axis_at), (shards_of,), jnp.float32, low / len(shards), high / len(shards))
        loudness = loudness * jnp.repeat(jnp.exp(heights), dims[axis_at] // shards_of).reshape((-1,) + (1,) * (len(dims) - 1 - axis_at))
    return loudness


def scatter_about(own_key, extent, deviation, reach, split=(), kind=jnp.bfloat16):
    factor_of = block_scale(own_key, extent, split, -0.22, 0.18) if split else 1.0
    array = jax.random.normal(own_key, extent, jnp.float32) * deviation * factor_of
    return jnp.minimum(jnp.maximum(array, -reach), reach).astype(kind)


def setup_inputs(seed: int = 0) -> dict:
    arg_keys = jax.random.split(jax.random.key(seed), 6)
    activations = draw_activations(jax.random.fold_in(arg_keys[5], 71), 0)
    cotangent = draw_cotangent(jax.random.fold_in(arg_keys[5], 71), 0)
    weight = scatter_about(arg_keys[2], (D, KV), D ** -0.5, 0.125)
    master = scatter_about(arg_keys[3], (D, KV), 0.1, 1.5, ((0, 32),), jnp.float32)
    momentum = scatter_about(arg_keys[4], (D, KV), 1.0, 6.0, ((0, 32),), jnp.float32)
    return dict(activations=activations, cotangent=cotangent, weight=weight, master=master, momentum=momentum)


def adasum_pair(lower, upper):
    lower_sq = jnp.sum(lower * lower)
    upper_sq = jnp.sum(upper * upper)
    cross = jnp.sum(lower * upper)
    return (1.0 - cross / (2.0 * (lower_sq + 1e-6))) * lower + (1.0 - cross / (2.0 * (upper_sq + 1e-6))) * upper


def reference(activations, cotangent, weight, master, momentum):
    group_rows = TOK_DEV * N_SUB
    scale = 1.0 / (group_rows ** 0.5)
    acts = activations.reshape(N_GRP, group_rows, D)
    cots = cotangent.reshape(N_GRP, group_rows, KV)

    def back_input(cot):
        return lax.dot_general(cot, weight, (((1,), (1,)), ((), ())), preferred_element_type=jnp.float32).astype(jnp.bfloat16)

    input_grad = lax.map(back_input, cots).reshape(N_GRP * group_rows, D)

    def back_weight(pair):
        return lax.dot_general(pair[0], pair[1], (((0,), (0,)), ((), ())), preferred_element_type=jnp.float32) * scale

    grads = lax.map(back_weight, (acts, cots))
    nodes = [grads[index] for index in range(N_GRP)]
    while len(nodes) > 1:
        nodes = [adasum_pair(nodes[2 * index], nodes[2 * index + 1]) for index in range(len(nodes) // 2)]
    combined = nodes[0]
    new_momentum = 0.9 * momentum + combined
    new_master = master - 0.05 * new_momentum
    new_weight = new_master.astype(jnp.bfloat16)
    return input_grad, new_momentum, new_master, new_weight
```

```python
import functools
import math

import jax
import jax.numpy as jnp
from jax import lax
from jax.experimental import pallas as pl
from jax.experimental.pallas import tpu as pltpu
from jax.sharding import PartitionSpec as P


LANES = 128
F16_MAX = 65504.0
INPUT_MAX = 16.0
F32 = jnp.float32


def flip(index, mask, bits):
    out = 0
    for bit in range(bits):
        value = index // 2**bit % 2
        out = out + 2**bit * (1 - value if mask >> bit & 1 else value)
    return out


def exchange(value, axis, mask):
    size = lax.axis_size(axis)
    return lax.ppermute(value, axis, [(source, source ^ mask) for source in range(size)])


def gram_kernel(n_grp, grp_bits, unscale, *refs):
    nodes, out_ref = refs[:-1], refs[-1]
    grp = lax.axis_index("grp")
    lane = lax.broadcasted_iota(jnp.int32, (1, LANES), 1)
    row = jnp.zeros((1, LANES), F32)
    values = [ref[...] for ref in nodes]
    for first in range(n_grp):
        for second in range(first, n_grp):
            product = values[first] * values[second]
            total = jnp.sum(jnp.sum(product, axis=0, keepdims=True), axis=1, keepdims=True)
            a = flip(grp, first, grp_bits)
            b = flip(grp, second, grp_bits)
            hit = (lane == a * n_grp + b) | (lane == b * n_grp + a)
            row = row + jnp.where(hit, total * unscale, 0.0)
    out_ref[...] = jnp.broadcast_to(row[None], out_ref.shape)


def tree_weights(gram, n_grp):
    nodes = [{g: None} for g in range(n_grp)]

    def times(weight, value):
        return value if weight is None else weight * value

    def inner(a, b):
        total = 0.0
        for g, wg in a.items():
            part = 0.0
            for h, wh in b.items():
                part = part + times(wh, gram[g][h])
            total = total + times(wg, part)
        return total

    while len(nodes) > 1:
        merged = []
        for low, high in zip(nodes[::2], nodes[1::2]):
            cross = inner(low, high)
            low_scale = 1.0 - cross / (2.0 * (inner(low, low) + 1e-06))
            high_scale = 1.0 - cross / (2.0 * (inner(high, high) + 1e-06))
            node = {g: times(w, low_scale) for g, w in low.items()}
            node.update({g: times(w, high_scale) for g, w in high.items()})
            merged.append(node)
        nodes = merged
    return nodes[0]


def update_kernel(n_grp, grp_bits, unscale, *refs):
    gram_ref, master_ref, momentum_ref = refs[:3]
    node_refs = refs[3 : 3 + n_grp]
    momentum_out, master_out, weight_out = refs[3 + n_grp :]
    grp = lax.axis_index("grp")
    row = jnp.sum(gram_ref[...], axis=0)
    lane = lax.broadcasted_iota(jnp.int32, (1, LANES), 1)
    gram = [
        [
            jnp.sum(jnp.where(lane == g * n_grp + h, row, 0.0), axis=1, keepdims=True)
            for h in range(n_grp)
        ]
        for g in range(n_grp)
    ]
    weights = tree_weights(gram, n_grp)
    combined = 0.0
    for mask, ref in enumerate(node_refs):
        group = flip(grp, mask, grp_bits)
        weight = sum(jnp.where(group == g, weights[g], 0.0) for g in range(n_grp))
        combined = combined + (weight * unscale) * ref[...]
    new_momentum = 0.9 * momentum_ref[...] + combined
    new_master = master_ref[...] - 0.05 * new_momentum
    momentum_out[...] = new_momentum
    master_out[...] = new_master
    weight_out[...] = new_master.astype(jnp.bfloat16)


def place_kernel(spots, n_sub, grp_bits, sub_bits, block, piece_ref, *refs):
    out_ref, sems = refs[-2], refs[-1]
    grp, sub = lax.axis_index("grp"), lax.axis_index("sub")
    copies = []
    for i, (d, e) in enumerate(spots):
        index = flip(grp, d, grp_bits) * n_sub + flip(sub, e, sub_bits)
        start = pl.multiple_of(index * block, block)
        copies.append(
            pltpu.make_async_copy(piece_ref.at[i], out_ref.at[pl.ds(start, block)], sems.at[i])
        )
    for copy in copies:
        copy.start()
    for copy in copies:
        copy.wait()


def place(out, piece, spots, rows, n_sub, grp_bits, sub_bits):
    count, block, width = piece.shape
    any_space = pl.BlockSpec(memory_space=pl.ANY)
    operands = (piece,) if out is None else (piece, out)
    return pl.pallas_call(
        functools.partial(place_kernel, spots, n_sub, grp_bits, sub_bits, block),
        out_shape=jax.ShapeDtypeStruct((rows, width), piece.dtype),
        in_specs=[pl.BlockSpec(memory_space=pltpu.VMEM)] + [any_space] * (len(operands) - 1),
        out_specs=any_space,
        scratch_shapes=[pltpu.SemaphoreType.DMA((count,))],
        input_output_aliases={} if out is None else {1: 0},
        name="place",
    )(*operands)


def body(activations, cotangent, weight, master, momentum):
    n_grp = lax.axis_size("grp")
    n_sub = lax.axis_size("sub")
    grp_bits, sub_bits = n_grp.bit_length() - 1, n_sub.bit_length() - 1
    tokens, width = activations.shape
    kv_width = cotangent.shape[1]
    block = width // (n_grp * n_sub)
    group_rows = tokens * n_sub
    bound = INPUT_MAX * INPUT_MAX * math.sqrt(group_rows)
    lift = 2.0 ** math.floor(math.log2(F16_MAX / bound))
    scale = lift / math.sqrt(group_rows)
    grp, sub = lax.axis_index("grp"), lax.axis_index("sub")

    nodes = [None] * n_grp
    columns = width // n_grp
    masks = sorted(range(1, n_grp), key=lambda m: -bin(m).count("1")) + [0]
    for turn, mask in enumerate(masks):
        owner = grp ^ mask
        lhs = lax.dynamic_slice_in_dim(activations, owner * columns, columns, axis=1)
        chunk = lax.dot_general(
            lhs, cotangent, (((0,), (0,)), ((), ())), preferred_element_type=F32
        )
        chunk = (chunk * scale).reshape((2,) * sub_bits + (block, kv_width))
        rest = list(range(1, sub_bits))
        if turn % 2:
            rest = rest[::-1]
        order = [0] + rest
        left = list(range(sub_bits))[::-1]
        for bit in order:
            axis = left.index(bit)
            mine = sub >> bit & 1
            keep = lax.dynamic_index_in_dim(chunk, mine, axis, keepdims=False)
            send = lax.dynamic_index_in_dim(chunk, 1 - mine, axis, keepdims=False)
            if bit == order[0]:
                chunk = keep + exchange(send, "sub", 2**bit)
            else:
                received = exchange(send.astype(jnp.float16), "sub", 2**bit)
                chunk = keep + received.astype(F32)
            left.remove(bit)
        nodes[mask] = exchange(chunk, "grp", mask) if mask else chunk

    vmem = pl.BlockSpec(memory_space=pltpu.VMEM)
    n_dev = n_grp * n_sub
    partial_gram = pl.pallas_call(
        functools.partial(gram_kernel, n_grp, grp_bits, 1.0 / (lift * lift)),
        out_shape=jax.ShapeDtypeStruct((n_dev, 1, LANES), F32),
        in_specs=[vmem] * n_grp,
        out_specs=vmem,
        name="gram",
    )(*nodes)
    grams = lax.all_to_all(partial_gram, ("grp", "sub"), 0, 0, tiled=True)

    shape = jax.ShapeDtypeStruct((block, kv_width), F32)
    new_momentum, new_master, own_weight = pl.pallas_call(
        functools.partial(update_kernel, n_grp, grp_bits, 1.0 / lift),
        out_shape=(shape, shape, jax.ShapeDtypeStruct((block, kv_width), jnp.bfloat16)),
        in_specs=[vmem] * (3 + n_grp),
        out_specs=(vmem,) * 3,
        name="update",
    )(grams, master, momentum, *nodes)

    cotangent, own_weight = lax.optimization_barrier((cotangent, own_weight))
    input_grad = lax.dot_general(
        cotangent, weight, (((1,), (1,)), ((), ())), preferred_element_type=F32
    ).astype(jnp.bfloat16)

    own = own_weight[None]
    by_grp = [own] + [exchange(own, "grp", d) for d in range(1, n_grp)]
    half = n_grp // 2
    pieces = []
    for turn, ds in enumerate((range(half), range(half, n_grp))):
        held = jnp.concatenate([by_grp[d] for d in ds], axis=0)
        spots = [(d, 0) for d in ds]
        rest = list(range(1, sub_bits))
        for bit in rest[::-1] if turn else rest:
            received = exchange(held, "sub", 2**bit)
            held = jnp.concatenate([held, received], axis=0)
            spots = spots + [(d, e ^ 2**bit) for d, e in spots]
        pieces.append((held, spots))
        pieces.append((exchange(held, "sub", 1), [(d, e ^ 1) for d, e in spots]))
    new_weight = None
    for piece, spots in pieces:
        new_weight = place(new_weight, piece, spots, width, n_sub, grp_bits, sub_bits)
    return input_grad, new_momentum, new_master, new_weight


def solution(mesh):
    rows = P(("grp", "sub"), None)
    return jax.shard_map(
        body,
        mesh=mesh,
        in_specs=(rows, rows, P(), rows, rows),
        out_specs=(rows, rows, rows, P()),
        check_vma=False,
    )
```

```python
import functools
import math

import jax
import jax.numpy as jnp
from jax import lax
from jax.experimental import pallas as pl
from jax.experimental.pallas import tpu as pltpu
from jax.sharding import PartitionSpec as P


LANES = 128
TILE = 256
F16_MAX = 65504.0
INPUT_MAX = 16.0
F32 = jnp.float32


def flip(index, mask, bits):
    out = 0
    for bit in range(bits):
        value = index // 2**bit % 2
        out = out + 2**bit * (1 - value if mask >> bit & 1 else value)
    return out


def exchange(value, even, odd=None):
    n_sub = lax.axis_size("sub")
    pairs = []
    for source in range(lax.axis_size("grp") * n_sub):
        d, e = even if odd is None or source % 2 == 0 else odd
        pairs.append((source, source ^ (d * n_sub + e)))
    return lax.ppermute(value, ("grp", "sub"), pairs)


def in_vmem(*values):
    return [pltpu.with_memory_space_constraint(v, pltpu.VMEM) for v in values]


def params(mib):
    return pltpu.CompilerParams(vmem_limit_bytes=mib * 2**20)


def product_kernel(mask, grp_bits, sub_bits, scale, tile, lhs_ref, rhs_ref, send_ref, keep_ref):
    pairs, block, width = keep_ref.shape
    columns = 2 * pairs * block
    owner = flip(lax.axis_index("grp"), mask, grp_bits)
    sub = lax.axis_index("sub")
    even = sub % 2 == 0
    lhs = lhs_ref[:, pl.ds(pl.multiple_of(owner * columns, columns), columns)]
    places = []
    for pair in range(pairs):
        apart = flip(sub // 2, pair, sub_bits - 1)
        bits = [apart // 2**i % 2 for i in range(sub_bits - 1)]
        rising = sum(2**i * bit for i, bit in enumerate(bits))
        falling = sum(2**i * bit for i, bit in enumerate(bits[::-1]))
        places.append((jnp.where(even, falling, rising), jnp.where(even, rising, falling)))
    for at in range(0, width, tile):
        part = lax.dot_general(
            lhs, rhs_ref[:, at : at + tile], (((0,), (0,)), ((), ())), preferred_element_type=F32
        )
        part = (part * scale).reshape(pairs, 2, block, tile)
        for pair, (mine, theirs) in enumerate(places):
            first, second = part[pair, 0], part[pair, 1]
            send_ref[theirs, :, at : at + tile] = jnp.where(even, second, first)
            keep_ref[mine, :, at : at + tile] = jnp.where(even, first, second)


def product(lhs, rhs, mask, grp_bits, sub_bits, block, scale):
    tokens, kv_width = rhs.shape
    vmem = pl.BlockSpec(memory_space=pltpu.VMEM)
    half = pltpu.VMEM((2**sub_bits // 2, block, kv_width), F32)
    columns = 2**sub_bits * block
    return pl.pallas_call(
        functools.partial(
            product_kernel, mask, grp_bits, sub_bits, scale, min(TILE, kv_width)
        ),
        out_shape=(half, half),
        in_specs=[vmem, vmem],
        out_specs=(vmem, vmem),
        cost_estimate=pl.CostEstimate(
            flops=2 * tokens * columns * kv_width,
            bytes_accessed=2 * tokens * (columns + kv_width) + 4 * columns * kv_width,
            transcendentals=0,
        ),
        compiler_params=params(12),
        name="product",
    )(*in_vmem(lhs, rhs))


def gram_kernel(n_grp, grp_bits, unscale, *refs):
    nodes, out_ref = refs[:-1], refs[-1]
    grp = lax.axis_index("grp")
    lane = lax.broadcasted_iota(jnp.int32, (1, LANES), 1)
    row = jnp.zeros((1, LANES), F32)
    values = [ref[...] for ref in nodes]
    for first in range(n_grp):
        for second in range(first, n_grp):
            product = values[first] * values[second]
            total = jnp.sum(jnp.sum(product, axis=0, keepdims=True), axis=1, keepdims=True)
            a = flip(grp, first, grp_bits)
            b = flip(grp, second, grp_bits)
            hit = (lane == a * n_grp + b) | (lane == b * n_grp + a)
            row = row + jnp.where(hit, total * unscale, 0.0)
    out_ref[...] = jnp.broadcast_to(row[None], out_ref.shape)


def tree_weights(gram, n_grp):
    nodes = [{g: None} for g in range(n_grp)]

    def times(weight, value):
        return value if weight is None else weight * value

    def inner(a, b):
        total = 0.0
        for g, wg in a.items():
            part = 0.0
            for h, wh in b.items():
                part = part + times(wh, gram[g][h])
            total = total + times(wg, part)
        return total

    while len(nodes) > 1:
        merged = []
        for low, high in zip(nodes[::2], nodes[1::2]):
            cross = inner(low, high)
            low_scale = 1.0 - cross / (2.0 * (inner(low, low) + 1e-06))
            high_scale = 1.0 - cross / (2.0 * (inner(high, high) + 1e-06))
            node = {g: times(w, low_scale) for g, w in low.items()}
            node.update({g: times(w, high_scale) for g, w in high.items()})
            merged.append(node)
        nodes = merged
    return nodes[0]


def update_kernel(n_grp, grp_bits, unscale, *refs):
    gram_ref, master_ref, momentum_ref = refs[:3]
    node_refs = refs[3 : 3 + n_grp]
    momentum_out, master_out, weight_out = refs[3 + n_grp :]
    grp = lax.axis_index("grp")
    row = jnp.sum(gram_ref[...], axis=0)
    lane = lax.broadcasted_iota(jnp.int32, (1, LANES), 1)
    gram = [
        [
            jnp.sum(jnp.where(lane == g * n_grp + h, row, 0.0), axis=1, keepdims=True)
            for h in range(n_grp)
        ]
        for g in range(n_grp)
    ]
    weights = tree_weights(gram, n_grp)
    combined = 0.0
    for mask, ref in enumerate(node_refs):
        group = flip(grp, mask, grp_bits)
        weight = sum(jnp.where(group == g, weights[g], 0.0) for g in range(n_grp))
        combined = combined + (weight * unscale) * ref[...]
    new_momentum = 0.9 * momentum_ref[...] + combined
    new_master = master_ref[...] - 0.05 * new_momentum
    momentum_out[...] = new_momentum
    master_out[...] = new_master
    weight_out[...] = new_master.astype(jnp.bfloat16)


def place_kernel(spots, n_sub, grp_bits, sub_bits, block, *refs):
    pieces, out_ref, sems = refs[: len(spots)], refs[-2], refs[-1]
    grp, sub = lax.axis_index("grp"), lax.axis_index("sub")
    odd = sub % 2
    copies = []
    for piece_ref, names in zip(pieces, spots):
        for i, both in enumerate(names):
            index = [flip(grp, d, grp_bits) * n_sub + flip(sub, e, sub_bits) for d, e in both]
            start = (index[0] + odd * (index[1] - index[0])) * block
            rows = out_ref.at[pl.ds(pl.multiple_of(start, block), block)]
            copies.append(pltpu.make_async_copy(piece_ref.at[i], rows, sems.at[len(copies)]))
    for copy in copies:
        copy.start()
    for copy in copies:
        copy.wait()


def place(out, pieces, rows, n_sub, grp_bits, sub_bits):
    stacks = [stack for stack, _ in pieces]
    spots = [names for _, names in pieces]
    _, block, width = stacks[0].shape
    any_space = pl.BlockSpec(memory_space=pltpu.HBM)
    vmem = pl.BlockSpec(memory_space=pltpu.VMEM)
    kept = [] if out is None else [out]
    return pl.pallas_call(
        functools.partial(place_kernel, spots, n_sub, grp_bits, sub_bits, block),
        out_shape=jax.ShapeDtypeStruct((rows, width), stacks[0].dtype),
        in_specs=[vmem] * len(stacks) + [any_space] * len(kept),
        out_specs=any_space,
        scratch_shapes=[pltpu.SemaphoreType.DMA((sum(map(len, spots)),))],
        input_output_aliases={len(stacks): 0} if kept else {},
        compiler_params=params(1),
        name="place",
    )(*in_vmem(*stacks), *kept)


def body(activations, cotangent, weight, master, momentum):
    n_grp = lax.axis_size("grp")
    n_sub = lax.axis_size("sub")
    grp_bits, sub_bits = n_grp.bit_length() - 1, n_sub.bit_length() - 1
    tokens, width = activations.shape
    kv_width = cotangent.shape[1]
    block = width // (n_grp * n_sub)
    group_rows = tokens * n_sub
    bound = INPUT_MAX * INPUT_MAX * math.sqrt(group_rows)
    lift = 2.0 ** math.floor(math.log2(F16_MAX / bound))
    scale = lift / math.sqrt(group_rows)

    grp_links = [2 ** (i + 1) - 1 for i in range(grp_bits)]
    sub_links = [2**i for i in range(1, sub_bits)]

    masks = sorted(range(1, n_grp), key=lambda m: (-(m & -m), m)) + [0]
    hops = list(zip(sub_links, sub_links[::-1]))
    terms = {}

    def total(values):
        return functools.reduce(lambda a, b: a + b, [v.astype(F32) for v in values])

    def step(mask):
        half = terms[mask][0].shape[0] // 2
        send = total([v[half:] for v in terms[mask]]).astype(jnp.float16)
        terms[mask] = [v[:half] for v in terms[mask]]
        return send

    def land(mask, hop, send):
        even, odd = hops[hop]
        terms[mask].append(exchange(send, (0, even), (0, odd)))

    for turn, mask in enumerate(masks):
        lhs = activations
        if turn >= 2:
            ahead = masks[turn - 2]
            send = step(ahead)
            lhs, send = lax.optimization_barrier((lhs, send))
            land(ahead, 0, send)
        away, kept = product(lhs, cotangent, mask, grp_bits, sub_bits, block, scale)
        terms[mask] = [kept, exchange(away, (0, 1))]
    for mask in masks[max(0, n_grp - 2) :]:
        land(mask, 0, step(mask))
    for hop in range(1, len(hops)):
        for mask in masks:
            land(mask, hop, step(mask))
    nodes = [None] * n_grp
    for mask in masks:
        node = total(terms[mask])[0]
        nodes[mask] = exchange(node, (mask, 0)) if mask else node

    vmem = pl.BlockSpec(memory_space=pltpu.VMEM)
    n_dev = n_grp * n_sub
    partial_gram = pl.pallas_call(
        functools.partial(gram_kernel, n_grp, grp_bits, 1.0 / (lift * lift)),
        out_shape=pltpu.VMEM((n_dev, 1, LANES), F32),
        in_specs=[vmem] * n_grp,
        out_specs=vmem,
        compiler_params=params(4),
        name="gram",
    )(*in_vmem(*nodes))
    grams = lax.all_to_all(partial_gram, ("grp", "sub"), 0, 0, tiled=True)

    shape = jax.ShapeDtypeStruct((block, kv_width), F32)
    new_momentum, new_master, own_weight = pl.pallas_call(
        functools.partial(update_kernel, n_grp, grp_bits, 1.0 / lift),
        out_shape=(shape, shape, pltpu.VMEM((block, kv_width), jnp.bfloat16)),
        in_specs=[vmem] * (3 + n_grp),
        out_specs=(vmem,) * 3,
        compiler_params=params(4),
        name="update",
    )(*in_vmem(grams, master, momentum, *nodes))

    even_links = [(d, 0) for d in grp_links] + [(0, e) for e in sub_links]
    odd_links = [(d, 0) for d in grp_links[::-1]] + [(0, e) for e in sub_links[::-1]]
    held = own_weight[None]
    for even, odd in list(zip(even_links, odd_links))[:-1]:
        held = jnp.concatenate([held, exchange(held, even, odd)], axis=0)
    came = exchange(held, even_links[-1], odd_links[-1])

    def spots_of(first, flipped):
        spots = []
        for i in range(first, first + held.shape[0]):
            both = []
            for links in (even_links, odd_links)[:: -1 if flipped else 1]:
                d = e = 0
                for bit, (dd, ee) in enumerate(links):
                    if i >> bit & 1:
                        d, e = d ^ dd, e ^ ee
                both.append((d, e ^ flipped))
            spots.append(tuple(both))
        return spots

    cotangent, held = lax.optimization_barrier((cotangent, held))
    input_grad = lax.dot_general(
        cotangent, weight, (((1,), (1,)), ((), ())), preferred_element_type=F32
    ).astype(jnp.bfloat16)

    count = held.shape[0]
    early = [(held, spots_of(0, 0)), (exchange(held, (0, 1)), spots_of(0, 1))]
    new_weight = place(None, early, width, n_sub, grp_bits, sub_bits)
    new_weight = place(new_weight, [(came, spots_of(count, 0))], width, n_sub, grp_bits, sub_bits)
    last = [(exchange(came, (0, 1)), spots_of(count, 1))]
    new_weight = place(new_weight, last, width, n_sub, grp_bits, sub_bits)
    return input_grad, new_momentum, new_master, new_weight


def solution(mesh):
    rows = P(("grp", "sub"), None)
    return jax.shard_map(
        body,
        mesh=mesh,
        in_specs=(rows, rows, P(), rows, rows),
        out_specs=(rows, rows, rows, P()),
        check_vma=False,
    )
```

```python
import functools
import math

import jax
import jax.numpy as jnp
from jax import lax
from jax.experimental import pallas as pl
from jax.experimental.pallas import tpu as pltpu
from jax.sharding import PartitionSpec as P


LANES = 128
TILE = 256
F16_MAX = 65504.0
INPUT_MAX = 16.0
F32 = jnp.float32


def flip(index, mask, bits):
    out = 0
    for bit in range(bits):
        value = index // 2**bit % 2
        out = out + 2**bit * (1 - value if mask >> bit & 1 else value)
    return out


def exchange(value, even, odd=None):
    n_sub = lax.axis_size("sub")
    pairs = []
    for source in range(lax.axis_size("grp") * n_sub):
        d, e = even if odd is None or source % 2 == 0 else odd
        pairs.append((source, source ^ (d * n_sub + e)))
    return lax.ppermute(value, ("grp", "sub"), pairs)


def in_vmem(*values):
    return [pltpu.with_memory_space_constraint(v, pltpu.VMEM) for v in values]


def params(mib):
    return pltpu.CompilerParams(vmem_limit_bytes=mib * 2**20)


def product_kernel(mask, grp_bits, sub_bits, scale, tile, lhs_ref, rhs_ref, send_ref, keep_ref):
    pairs, block, width = keep_ref.shape
    columns = 2 * pairs * block
    owner = flip(lax.axis_index("grp"), mask, grp_bits)
    sub = lax.axis_index("sub")
    even = sub % 2 == 0
    lhs = lhs_ref[:, pl.ds(pl.multiple_of(owner * columns, columns), columns)]
    places = []
    for pair in range(pairs):
        apart = flip(sub // 2, pair, sub_bits - 1)
        bits = [apart // 2**i % 2 for i in range(sub_bits - 1)]
        rising = sum(2**i * bit for i, bit in enumerate(bits))
        falling = sum(2**i * bit for i, bit in enumerate(bits[::-1]))
        places.append((jnp.where(even, falling, rising), jnp.where(even, rising, falling)))
    for at in range(0, width, tile):
        part = lax.dot_general(
            lhs, rhs_ref[:, at : at + tile], (((0,), (0,)), ((), ())), preferred_element_type=F32
        )
        part = (part * scale).reshape(pairs, 2, block, tile)
        for pair, (mine, theirs) in enumerate(places):
            first, second = part[pair, 0], part[pair, 1]
            send_ref[theirs, :, at : at + tile] = jnp.where(even, second, first)
            keep_ref[mine, :, at : at + tile] = jnp.where(even, first, second)


def product(lhs, rhs, mask, grp_bits, sub_bits, block, scale):
    tokens, kv_width = rhs.shape
    vmem = pl.BlockSpec(memory_space=pltpu.VMEM)
    half = pltpu.VMEM((2**sub_bits // 2, block, kv_width), F32)
    columns = 2**sub_bits * block
    return pl.pallas_call(
        functools.partial(
            product_kernel, mask, grp_bits, sub_bits, scale, min(TILE, kv_width)
        ),
        out_shape=(half, half),
        in_specs=[vmem, vmem],
        out_specs=(vmem, vmem),
        cost_estimate=pl.CostEstimate(
            flops=2 * tokens * columns * kv_width,
            bytes_accessed=2 * tokens * (columns + kv_width) + 4 * columns * kv_width,
            transcendentals=0,
        ),
        compiler_params=params(12),
        name="product",
    )(*in_vmem(lhs, rhs))


def gram_kernel(n_grp, grp_bits, unscale, *refs):
    nodes, out_ref = refs[:-1], refs[-1]
    grp = lax.axis_index("grp")
    lane = lax.broadcasted_iota(jnp.int32, (1, LANES), 1)
    row = jnp.zeros((1, LANES), F32)
    values = [ref[...] for ref in nodes]
    for first in range(n_grp):
        for second in range(first, n_grp):
            product = values[first] * values[second]
            total = jnp.sum(jnp.sum(product, axis=0, keepdims=True), axis=1, keepdims=True)
            a = flip(grp, first, grp_bits)
            b = flip(grp, second, grp_bits)
            hit = (lane == a * n_grp + b) | (lane == b * n_grp + a)
            row = row + jnp.where(hit, total * unscale, 0.0)
    out_ref[...] = jnp.broadcast_to(row[None], out_ref.shape)


def tree_weights(gram, n_grp):
    nodes = [{g: None} for g in range(n_grp)]

    def times(weight, value):
        return value if weight is None else weight * value

    def inner(a, b):
        total = 0.0
        for g, wg in a.items():
            part = 0.0
            for h, wh in b.items():
                part = part + times(wh, gram[g][h])
            total = total + times(wg, part)
        return total

    while len(nodes) > 1:
        merged = []
        for low, high in zip(nodes[::2], nodes[1::2]):
            cross = inner(low, high)
            low_scale = 1.0 - cross / (2.0 * (inner(low, low) + 1e-06))
            high_scale = 1.0 - cross / (2.0 * (inner(high, high) + 1e-06))
            node = {g: times(w, low_scale) for g, w in low.items()}
            node.update({g: times(w, high_scale) for g, w in high.items()})
            merged.append(node)
        nodes = merged
    return nodes[0]


def update_kernel(n_grp, grp_bits, unscale, *refs):
    gram_ref, master_ref, momentum_ref = refs[:3]
    node_refs = refs[3 : 3 + n_grp]
    momentum_out, master_out, weight_out = refs[3 + n_grp :]
    grp = lax.axis_index("grp")
    row = jnp.sum(gram_ref[...], axis=0)
    lane = lax.broadcasted_iota(jnp.int32, (1, LANES), 1)
    gram = [
        [
            jnp.sum(jnp.where(lane == g * n_grp + h, row, 0.0), axis=1, keepdims=True)
            for h in range(n_grp)
        ]
        for g in range(n_grp)
    ]
    weights = tree_weights(gram, n_grp)
    combined = 0.0
    for mask, ref in enumerate(node_refs):
        group = flip(grp, mask, grp_bits)
        weight = sum(jnp.where(group == g, weights[g], 0.0) for g in range(n_grp))
        combined = combined + (weight * unscale) * ref[...]
    new_momentum = 0.9 * momentum_ref[...] + combined
    new_master = master_ref[...] - 0.05 * new_momentum
    momentum_out[...] = new_momentum
    master_out[...] = new_master
    weight_out[...] = new_master.astype(jnp.bfloat16)


def place_kernel(spots, block, grp_bits, sub_bits, *refs):
    pieces, out_ref, sems = refs[: len(spots)], refs[-2], refs[-1]
    grp, sub = lax.axis_index("grp"), lax.axis_index("sub")
    odd = sub % 2
    copies = []
    for piece_ref, names in zip(pieces, spots):
        count = piece_ref.shape[1]
        for i, (both, row) in enumerate(names):
            index = [
                flip(grp, d, grp_bits) * 2**sub_bits + flip(sub, e, sub_bits) for d, e in both
            ]
            start = (index[0] + odd * (index[1] - index[0])) * block + row
            rows = out_ref.at[pl.ds(pl.multiple_of(start, count), count)]
            copies.append(pltpu.make_async_copy(piece_ref.at[i], rows, sems.at[len(copies)]))
    for copy in copies:
        copy.start()
    for copy in copies:
        copy.wait()


def place(out, pieces, rows, block, grp_bits, sub_bits):
    stacks = [stack for stack, _ in pieces]
    spots = [names for _, names in pieces]
    width = stacks[0].shape[2]
    any_space = pl.BlockSpec(memory_space=pltpu.HBM)
    vmem = pl.BlockSpec(memory_space=pltpu.VMEM)
    kept = [] if out is None else [out]
    return pl.pallas_call(
        functools.partial(place_kernel, spots, block, grp_bits, sub_bits),
        out_shape=jax.ShapeDtypeStruct((rows, width), stacks[0].dtype),
        in_specs=[vmem] * len(stacks) + [any_space] * len(kept),
        out_specs=any_space,
        scratch_shapes=[pltpu.SemaphoreType.DMA((sum(map(len, spots)),))],
        input_output_aliases={len(stacks): 0} if kept else {},
        compiler_params=params(1),
        name="place",
    )(*in_vmem(*stacks), *kept)


def body(activations, cotangent, weight, master, momentum):
    n_grp = lax.axis_size("grp")
    n_sub = lax.axis_size("sub")
    grp_bits, sub_bits = n_grp.bit_length() - 1, n_sub.bit_length() - 1
    tokens, width = activations.shape
    kv_width = cotangent.shape[1]
    block = width // (n_grp * n_sub)
    group_rows = tokens * n_sub
    bound = INPUT_MAX * INPUT_MAX * math.sqrt(group_rows)
    lift = 2.0 ** math.floor(math.log2(F16_MAX / bound))
    scale = lift / math.sqrt(group_rows)

    grp_links = [2 ** (i + 1) - 1 for i in range(grp_bits)]
    sub_links = [2**i for i in range(1, sub_bits)]

    masks = sorted(range(1, n_grp), key=lambda m: (-(m & -m), m)) + [0]
    hops = list(zip(sub_links, sub_links[::-1]))
    terms = {}

    def total(values):
        return functools.reduce(lambda a, b: a + b, [v.astype(F32) for v in values])

    def step(mask):
        half = terms[mask][0].shape[0] // 2
        send = total([v[half:] for v in terms[mask]]).astype(jnp.float16)
        terms[mask] = [v[:half] for v in terms[mask]]
        return send

    def land(mask, hop, send):
        even, odd = hops[hop]
        terms[mask].append(exchange(send, (0, even), (0, odd)))

    for turn, mask in enumerate(masks):
        lhs = activations
        if turn >= 2:
            ahead = masks[turn - 2]
            send = step(ahead)
            lhs, send = lax.optimization_barrier((lhs, send))
            land(ahead, 0, send)
        away, kept = product(lhs, cotangent, mask, grp_bits, sub_bits, block, scale)
        terms[mask] = [kept, exchange(away, (0, 1))]
    for mask in masks[max(0, n_grp - 2) :]:
        send = step(mask)
        if mask == masks[-1]:
            first = terms[masks[0]]
            first[0], send = lax.optimization_barrier((first[0], send))
        land(mask, 0, send)
    for hop in range(1, len(hops)):
        for mask in masks:
            land(mask, hop, step(mask))
    nodes = [None] * n_grp
    for mask in masks:
        node = total(terms[mask])[0]
        nodes[mask] = exchange(node, (mask, 0)) if mask else node

    vmem = pl.BlockSpec(memory_space=pltpu.VMEM)
    n_dev = n_grp * n_sub
    partial_gram = pl.pallas_call(
        functools.partial(gram_kernel, n_grp, grp_bits, 1.0 / (lift * lift)),
        out_shape=pltpu.VMEM((n_dev, 1, LANES), F32),
        in_specs=[vmem] * n_grp,
        out_specs=vmem,
        compiler_params=params(4),
        name="gram",
    )(*in_vmem(*nodes))
    grams = lax.all_to_all(partial_gram, ("grp", "sub"), 0, 0, tiled=True)

    shape = jax.ShapeDtypeStruct((block, kv_width), F32)
    new_momentum, new_master, own_weight = pl.pallas_call(
        functools.partial(update_kernel, n_grp, grp_bits, 1.0 / lift),
        out_shape=(shape, shape, pltpu.VMEM((block, kv_width), jnp.bfloat16)),
        in_specs=[vmem] * (3 + n_grp),
        out_specs=(vmem,) * 3,
        compiler_params=params(4),
        name="update",
    )(*in_vmem(grams, master, momentum, *nodes))

    over_grp, over_sub = [(d, 0) for d in grp_links], [(0, e) for e in sub_links]
    even_orders = [over_grp + over_sub, over_sub + over_grp]
    odd_orders = [over_grp[::-1] + over_sub[::-1], over_sub[::-1] + over_grp[::-1]]
    part_rows = block // 2
    parts = [own_weight[None, :part_rows], own_weight[None, part_rows:]]
    hops = grp_bits + sub_bits - 1
    for hop in range(hops - 1):
        came = [exchange(p, even_orders[i][hop], odd_orders[i][hop]) for i, p in enumerate(parts)]
        parts = [jnp.concatenate(both, axis=0) for both in zip(parts, came)]
    came = [exchange(p, even_orders[i][-1], odd_orders[i][-1]) for i, p in enumerate(parts)]
    across = [exchange(p, (0, 1)) for p in parts]

    def spots_of(part, last, flipped):
        count = 2 ** (hops - 1)
        spots = []
        for i in range(last * count, (last + 1) * count):
            both = []
            for links in (even_orders[part], odd_orders[part])[:: -1 if flipped else 1]:
                d = e = 0
                for bit, (dd, ee) in enumerate(links):
                    if i >> bit & 1:
                        d, e = d ^ dd, e ^ ee
                both.append((d, e ^ flipped))
            spots.append((tuple(both), part * part_rows))
        return spots

    cotangent, parts[1] = lax.optimization_barrier((cotangent, parts[1]))
    input_grad = lax.dot_general(
        cotangent, weight, (((1,), (1,)), ((), ())), preferred_element_type=F32
    ).astype(jnp.bfloat16)
    early = [(parts[i], spots_of(i, 0, 0)) for i in range(2)]
    early += [(across[i], spots_of(i, 0, 1)) for i in range(2)]
    new_weight = place(None, early, width, block, grp_bits, sub_bits)
    came[0], came[1], input_grad, new_weight = lax.optimization_barrier((*came, input_grad, new_weight))
    last = [exchange(p, (0, 1)) for p in came]
    middle = [(came[i], spots_of(i, 1, 0)) for i in range(2)]
    new_weight = place(new_weight, middle, width, block, grp_bits, sub_bits)
    end = [(last[i], spots_of(i, 1, 1)) for i in range(2)]
    new_weight = place(new_weight, end, width, block, grp_bits, sub_bits)
    return input_grad, new_momentum, new_master, new_weight


def solution(mesh):
    rows = P(("grp", "sub"), None)
    return jax.shard_map(
        body,
        mesh=mesh,
        in_specs=(rows, rows, P(), rows, rows),
        out_specs=(rows, rows, rows, P()),
        check_vma=False,
    )
```
